32 devices in a mesh: wide: 16 (over z, x, core), narrow: 2 (over y).
Axes of the slice: x: 2, y: 2, z: 4, core: 2. Of those that a mesh axis runs over, the one named last changes fastest.
Arguments:
- inputs: bfloat16 [512, 8192], P('wide', 'narrow'), may hold values from -6 to 6
- out_grad: bfloat16 [512, 8192], P('wide', 'narrow'), may hold values from -6 to 6
- preact: bfloat16 [512, 32768], P('narrow', 'wide'), may hold values from -6 to 6
- w_up: bfloat16 [8192, 32768], P('narrow', 'wide'), may hold values from -0.0625 to 0.0625
- w_down: bfloat16 [32768, 8192], P('wide', 'narrow'), may hold values from -0.03125 to 0.03125
Outputs:
- in_grad: bfloat16 [512, 8192], P('wide', 'narrow')
- up_grad: bfloat16 [8192, 32768], P('narrow', 'wide')
- down_grad: bfloat16 [32768, 8192], P('wide', 'narrow')
The draws below stay inside these ranges and needn't reach their ends.
All inputs are finite; a program needn't handle non-finite values.
Results may differ from the reference program's by a relative error of at most 0.005.
Values may be sent and summed in bfloat16 or wider, within the bound.
A program may use at most 192 MiB of HBM per device.

```python
import math
import jax
import jax.numpy as jnp

D = 8192
F = 32768
TOKENS = 512


def spiked(entries, rng, source, target, blocks, factor):
    owner, partner = [(jnp.arange(entries.shape[position]) // (entries.shape[position] // blocks)).reshape([-1 if axis == position else 1 for axis in range(entries.ndim)]) for position in (source, target)]
    chosen = jax.random.permutation(rng, blocks)[partner]
    strong = (owner == chosen) | (owner == (partner + blocks // 2) % blocks)
    return jnp.where(strong, factor * entries, entries)


def level_of(key, extent, pieces, least, high):
    def one(position, blocks):
        steps = jax.random.uniform(jax.random.fold_in(jax.random.fold_in(key, 6), position), (blocks,), jnp.float32, least / len(pieces), high / len(pieces))
        return jnp.repeat(jnp.exp(steps), extent[position] // blocks).reshape((-1,) + (1,) * (len(extent) - position - 1))

    level = one(*pieces[0])
    for cut in pieces[1:]:
        level = level * one(*cut)
    return level


def gaussian(own_key, dims, width, limit, pieces=(), held_as=jnp.bfloat16):
    drawn = width * jax.random.normal(own_key, dims, jnp.float32)
    if pieces:
        drawn = drawn * level_of(own_key, dims, pieces, -0.22, 0.18)
    return jnp.clip(drawn, -limit, limit).astype(held_as)


def noise_with(rng, dims, spread, bound, split, heavy, held_as=jnp.bfloat16):
    array = spread * jax.random.normal(rng, dims, jnp.float32)
    if split:
        array = array * level_of(rng, dims, split, -0.22, 0.18)
    return jnp.clip(spiked(array, jax.random.fold_in(rng, 3), *heavy), -bound, bound).astype(held_as)


def setup_inputs(seed: int = 0) -> dict:
    splits = jax.random.split(jax.random.key(seed), 6)
    inputs = gaussian(splits[0], (TOKENS, D), 1.0, 6.0, ((0, 16), (1, 2)))
    out_grad = gaussian(splits[1], (TOKENS, D), 1.0, 6.0, ((0, 16), (1, 2)))
    preact = noise_with(splits[2], (TOKENS, F), 1.0, 6.0, ((0, 2), (1, 16)), (1, 0, 16, 2.0))
    w_up = gaussian(splits[3], (D, F), D ** -0.5, 0.0625, ((0, 2), (1, 16)))
    w_down = gaussian(splits[4], (F, D), F ** -0.5, 0.03125, ((0, 16), (1, 2)))
    return {"inputs": inputs, "out_grad": out_grad, "preact": preact, "w_up": w_up, "w_down": w_down}


def gelu_parts(pre):
    value = pre.astype(jnp.float32)
    cdf = 0.5 * (1.0 + jax.scipy.special.erf(value / math.sqrt(2.0)))
    dens = jnp.exp(-0.5 * value * value) / math.sqrt(2.0 * math.pi)
    return (value * cdf, cdf + value * dens)

def reference(inputs, out_grad, preact, w_up, w_down):
    act_grad = jnp.dot(out_grad, w_down.T, preferred_element_type=jnp.float32)
    activ_f, slope = gelu_parts(preact)
    activ = activ_f.astype(jnp.bfloat16)
    pre_grad = (act_grad * slope).astype(jnp.bfloat16)
    down_grad = jnp.dot(activ.T, out_grad, preferred_element_type=jnp.float32).astype(jnp.bfloat16)
    up_grad = jnp.dot(inputs.T, pre_grad, preferred_element_type=jnp.float32).astype(jnp.bfloat16)
    in_grad = jnp.dot(pre_grad, w_up.T, preferred_element_type=jnp.float32).astype(jnp.bfloat16)
    return (in_grad, up_grad, down_grad)
```

```python
import math

import jax
import jax.numpy as jnp
from jax import lax
from jax.experimental import pallas as pl
from jax.experimental.pallas import tpu as pltpu
from jax.sharding import PartitionSpec as P


F32 = jnp.float32
BF16 = jnp.bfloat16
CHUNKS = 2


def gelu_parts(pre):
    value = pre.astype(F32)
    cdf = 0.5 * (1.0 + lax.erf(value / math.sqrt(2.0)))
    dens = jnp.exp(-0.5 * value * value) / math.sqrt(2.0 * math.pi)
    return (value * cdf, cdf + value * dens)


def place(o, m, c):
    return (o * 2 + m) * 2 + c


def gather_wide(block, outer):
    wide = lax.axis_index("wide")
    o, m, c = wide // 4, (wide // 2) % 2, wide % 2
    rows, cols = block.shape

    def line(x, step, first, last):
        pairs = [
            (place(a, b, d), place(a + step, b, d))
            for a in range(first, last)
            for b in range(2)
            for d in range(2)
        ]
        return lax.ppermute(x, "wide", pairs)

    def cross(x, first, last):
        pairs = [
            (place(a, b, d), place(a, 1 - b, d))
            for a in range(first, last)
            for b in range(2)
            for d in range(2)
        ]
        return lax.ppermute(x, "wide", pairs)

    below, above = [block], [block]
    below_x = [cross(block, 0, outer)]
    above_x = [below_x[0]]
    for s in range(1, outer):
        below.append(line(below[-1], 1, s - 1, outer - 1))
        above.append(line(above[-1], -1, 1, outer - s + 1))
        below_x.append(cross(below[-1], s, outer))
        above_x.append(cross(above[-1], 0, outer - s))
    mine = jnp.zeros((outer, 2, rows, cols), block.dtype)
    for s in range(outer):
        for side, (lo, hi) in enumerate(((below, above), (below_x, above_x))):
            part = lo[s] if s == 0 else jnp.where(o >= s, lo[s], hi[outer - s])
            half = m if side == 0 else 1 - m
            mine = lax.dynamic_update_slice(
                mine, part[None, None], (lax.rem(o - s + outer, outer), half, 0, 0)
            )
    swap = [(i, i ^ 1) for i in range(4 * outer)]
    other = lax.ppermute(mine, "wide", swap)
    whole = jnp.where(
        c == 0, jnp.stack([mine, other], 2), jnp.stack([other, mine], 2)
    )
    return whole.reshape(4 * outer * rows, cols)


def shift_narrow(x, s, n):
    return lax.ppermute(x, "narrow", [(i, (i + s) % n) for i in range(n)])


def scatter_chunk(part, k, outer, per):
    wide = lax.axis_index("wide")
    o, m, c = wide // 4, (wide // 2) % 2, wide % 2
    rows, cols = part.shape[-2:]
    low = part.astype(BF16)
    keep = lax.dynamic_index_in_dim(part, c, 2, keepdims=False)
    give = lax.dynamic_index_in_dim(low, 1 - c, 2, keepdims=False)
    got = lax.ppermute(give, "wide", [(i, i ^ 1) for i in range(4 * outer)])
    chip = keep + got.astype(F32)
    keep = lax.dynamic_index_in_dim(chip, m, 1, keepdims=False)
    give = lax.dynamic_index_in_dim(chip.astype(BF16), 1 - m, 1, keepdims=False)
    got = lax.ppermute(give, "wide", [(i, i ^ 2) for i in range(4 * outer)])
    pair = keep + got.astype(F32)
    low = pair.astype(BF16)
    first = k * per
    total = lax.dynamic_index_in_dim(pair, jnp.clip(o - first, 0, per - 1), 0, keepdims=False)
    for s in range(1, outer):
        target = jnp.clip(lax.rem(o - s + outer, outer) - first, 0, per - 1)
        give = lax.dynamic_index_in_dim(low, target, 0, keepdims=False)
        pairs = [
            (place((d + s) % outer, a, b), place(d, a, b))
            for d in range(first, first + per)
            for a in range(2)
            for b in range(2)
        ]
        total = total + lax.ppermute(give, "wide", pairs).astype(F32)
    return total


def outer_product_kernel(a_ref, b_ref, o_ref):
    o_ref[...] = lax.dot_general(
        a_ref[...], b_ref[...], (((0,), (0,)), ((), ())), preferred_element_type=F32
    ).astype(BF16)


def outer_product(a, b):
    t, d = a.shape
    f = b.shape[1]
    tile = min(256, d)
    return pl.pallas_call(
        outer_product_kernel,
        grid=(d // tile,),
        in_specs=[
            pl.BlockSpec((t, tile), lambda i: (0, i)),
            pl.BlockSpec((t, f), lambda i: (0, 0)),
        ],
        out_specs=pl.BlockSpec((tile, f), lambda i: (i, 0)),
        out_shape=jax.ShapeDtypeStruct((d, f), BF16),
        compiler_params=pltpu.CompilerParams(vmem_limit_bytes=40 * 2**20),
        cost_estimate=pl.CostEstimate(
            flops=2 * t * d * f,
            bytes_accessed=2 * (t * d + t * f + d * f),
            transcendentals=0,
        ),
    )(a, b)


def shards(inputs, out_grad, preact, w_up, w_down):
    wide_n = lax.axis_size("wide")
    narrow_n = lax.axis_size("narrow")
    outer = wide_n // 4
    me = lax.axis_index("narrow")
    rows = preact.shape[0]
    tokens = rows * narrow_n

    pre_all = jnp.zeros((tokens, preact.shape[1]), preact.dtype)
    pre_all = lax.dynamic_update_slice(pre_all, preact, (me * rows, 0))
    for s in range(1, narrow_n):
        got = shift_narrow(preact, s, narrow_n)
        pre_all = lax.dynamic_update_slice(
            pre_all, got, (lax.rem(me - s + narrow_n, narrow_n) * rows, 0)
        )
    grad_all = gather_wide(out_grad, outer)

    span = tokens // CHUNKS
    acts = []
    for k in range(CHUNKS):
        part = lax.dot_general(
            grad_all[k * span : (k + 1) * span],
            w_down,
            (((1,), (1,)), ((), ())),
            preferred_element_type=F32,
        )
        low = part.astype(BF16)
        acts.append((part, [shift_narrow(low, s, narrow_n) for s in range(1, narrow_n)]))

    inputs_all = gather_wide(inputs, outer)
    activ = gelu_parts(pre_all)[0].astype(BF16)
    down_grad = outer_product(activ, grad_all)

    pgrads, totals = [], []
    per = outer // CHUNKS
    for k, (part, others) in enumerate(acts):
        act = part
        for other in others:
            act = act + other.astype(F32)
        slope = gelu_parts(pre_all[k * span : (k + 1) * span])[1]
        pgrad = (act * slope).astype(BF16)
        pgrads.append(pgrad)
        prod = lax.dot_general(
            pgrad, w_up, (((1,), (1,)), ((), ())), preferred_element_type=F32
        )
        totals.append(
            scatter_chunk(prod.reshape(per, 2, 2, -1, prod.shape[1]), k, outer, per)
        )
    up_grad = outer_product(inputs_all, jnp.concatenate(pgrads, 0))
    o = lax.axis_index("wide") // 4
    in_grad = totals[0]
    for k in range(1, CHUNKS):
        in_grad = jnp.where(o >= k * per, totals[k], in_grad)
    return (in_grad.astype(BF16), up_grad, down_grad)


def solution(mesh):
    in_specs = (
        P("wide", "narrow"),
        P("wide", "narrow"),
        P("narrow", "wide"),
        P("narrow", "wide"),
        P("wide", "narrow"),
    )
    out_specs = (P("wide", "narrow"), P("narrow", "wide"), P("wide", "narrow"))
    return jax.shard_map(shards, mesh=mesh, in_specs=in_specs, out_specs=out_specs, check_vma=False)
```

```python
import functools
import math

import jax
import jax.numpy as jnp
from jax import lax
from jax.experimental import pallas as pl
from jax.experimental.pallas import tpu as pltpu
from jax.sharding import PartitionSpec as P


F32 = jnp.float32
BF16 = jnp.bfloat16
CHUNKS = 2


def gelu_parts(pre):
    value = pre.astype(F32)
    cdf = 0.5 * (1.0 + lax.erf(value / math.sqrt(2.0)))
    dens = jnp.exp(-0.5 * value * value) / math.sqrt(2.0 * math.pi)
    return (value * cdf, cdf + value * dens)


def place(o, m, c):
    return (o * 2 + m) * 2 + c


def relay(own, whole, sends, recvs, outer, pending):
    wide = lax.axis_index("wide")
    o, m, c = wide // 4, (wide // 2) % 2, wide % 2
    rows = own.shape[0]
    steps = 2 * outer - 1

    def at(oo, mm, cc):
        return whole.at[pl.ds(pl.multiple_of(place(oo, mm, cc) * rows, rows), rows)]

    def send(src, dst, slot, device, valid=None):
        copy = pltpu.make_async_remote_copy(
            src_ref=src,
            dst_ref=dst,
            send_sem=sends.at[slot],
            recv_sem=recvs.at[slot],
            device_id={"wide": device},
            device_id_type=pl.DeviceIdType.MESH,
        )
        if valid is None:
            copy.start()
        else:
            pl.when(valid)(copy.start)
        pending.append((copy, valid))

    def arrived(dst, slot, valid=None):
        copy = pltpu.make_async_remote_copy(
            src_ref=dst,
            dst_ref=dst,
            send_sem=sends.at[slot],
            recv_sem=recvs.at[slot],
            device_id={"wide": place(o, m, 1 - c)},
            device_id_type=pl.DeviceIdType.MESH,
        )
        if valid is None:
            copy.wait_recv()
        else:
            pl.when(valid)(copy.wait_recv)

    def spread(src, oo, index, valid):
        send(src, at(oo, m, c), steps + index, place(o, 1 - m, c), valid)
        send(src, at(oo, m, c), 2 * steps + index, place(o, m, 1 - c), valid)

    def crossed(oo, index, valid):
        arrived(at(oo, 1 - m, c), steps + index, valid)
        send(at(oo, 1 - m, c), at(oo, 1 - m, c), 3 * steps + index, place(o, m, 1 - c), valid)

    send(own, at(o, m, c), 1, jnp.minimum(o + 1, outer - 1) * 4 + m * 2 + c, o + 1 < outer)
    send(own, at(o, m, c), outer, jnp.maximum(o - 1, 0) * 4 + m * 2 + c, o >= 1)
    spread(own, o, 0, None)
    yield
    blocks = [(o, 0, None)]
    for s in range(1, outer):
        for up in (True, False):
            oo = jnp.maximum(o - s, 0) if up else jnp.minimum(o + s, outer - 1)
            valid = o >= s if up else o + s < outer
            index = s if up else outer - 1 + s
            arrived(at(oo, m, c), index, valid)
            if s + 1 < outer:
                if up:
                    onward = jnp.logical_and(valid, o + 1 < outer)
                    target = jnp.minimum(o + 1, outer - 1)
                else:
                    onward = jnp.logical_and(valid, o >= 1)
                    target = jnp.maximum(o - 1, 0)
                send(at(oo, m, c), at(oo, m, c), index + 1, place(target, m, c), onward)
            spread(at(oo, m, c), oo, index, valid)
            blocks.append((oo, index, valid))
        if s == 1:
            crossed(*blocks[0])
        else:
            crossed(*blocks[2 * s - 3])
            crossed(*blocks[2 * s - 2])
        yield
    for oo, index, valid in blocks[2 * outer - 3 :]:
        crossed(oo, index, valid)
    yield
    for oo, index, valid in blocks:
        arrived(at(oo, m, 1 - c), 2 * steps + index, valid)
        arrived(at(oo, 1 - m, 1 - c), 3 * steps + index, valid)


def entry_kernel(
    outer, narrow_n, g_ref, i_ref, p_ref, w_ref, grad_all, inputs_all, pre_all, part_ref, low_ref,
    w_vmem, sends, recvs, narrow_send, narrow_recv, local
):
    wide, me = lax.axis_index("wide"), lax.axis_index("narrow")
    o, m, c = wide // 4, (wide // 2) % 2, wide % 2
    rows, span = g_ref.shape[0], p_ref.shape[0]
    copies = [
        pltpu.make_async_copy(w_ref, w_vmem, local.at[0]),
        pltpu.make_async_copy(
            g_ref, grad_all.at[pl.ds(pl.multiple_of(wide * rows, rows), rows)], local.at[1]
        ),
        pltpu.make_async_copy(
            i_ref, inputs_all.at[pl.ds(pl.multiple_of(wide * rows, rows), rows)], local.at[2]
        ),
        pltpu.make_async_copy(
            p_ref, pre_all.at[pl.ds(pl.multiple_of(me * span, span), span)], local.at[3]
        ),
    ]
    for copy in copies:
        copy.start()

    barrier = pltpu.get_barrier_semaphore()

    def greet(device):
        pl.semaphore_signal(
            barrier, inc=1, device_id=device, device_id_type=pl.DeviceIdType.MESH
        )

    greet({"wide": place(o, 1 - m, c)})
    greet({"wide": place(o, m, 1 - c)})
    for s in range(1, narrow_n):
        greet({"narrow": lax.rem(me + s, narrow_n)})
    pl.when(o + 1 < outer)(lambda: greet({"wide": place(jnp.minimum(o + 1, outer - 1), m, c)}))
    pl.when(o >= 1)(lambda: greet({"wide": place(jnp.maximum(o - 1, 0), m, c)}))
    pl.semaphore_wait(
        barrier, 1 + narrow_n + jnp.minimum(o, 1) + jnp.minimum(outer - 1 - o, 1)
    )

    pending = []
    first = relay(g_ref, grad_all, sends.at[0], recvs.at[0], outer, pending)
    next(first)
    swaps = []
    for s in range(1, narrow_n):
        swap = pltpu.make_async_remote_copy(
            src_ref=p_ref,
            dst_ref=pre_all.at[pl.ds(pl.multiple_of(me * span, span), span)],
            send_sem=narrow_send.at[s],
            recv_sem=narrow_recv.at[s],
            device_id={"narrow": lax.rem(me + s, narrow_n)},
            device_id_type=pl.DeviceIdType.MESH,
        )
        swap.start()
        swaps.append(swap)
    for _ in range(outer - 1):
        next(first)
    second = relay(i_ref, inputs_all, sends.at[1], recvs.at[1], outer, pending)
    next(second)
    for _ in first:
        pass
    copies[0].wait()
    copies[1].wait()

    tile = 256
    tiles = w_vmem.shape[0] // tile
    edges = [tiles * k // (outer + 1) for k in range(outer + 2)]
    for lo, hi in zip(edges[:-1], edges[1:]):

        def piece(j, carry):
            part = pl.ds(pl.multiple_of(j * tile, tile), tile)
            value = lax.dot_general(
                grad_all[...], w_vmem[part, :], (((1,), (1,)), ((), ())),
                preferred_element_type=F32,
            )
            part_ref[:, part] = value
            low_ref[:, part] = value.astype(BF16)
            return carry

        if hi > lo:
            lax.fori_loop(lo, hi, piece, 0)
        next(second, None)
    for _ in second:
        pass
    for copy, valid in pending:
        if valid is None:
            copy.wait_send()
        else:
            pl.when(valid)(copy.wait_send)
    for swap in swaps:
        swap.wait()
    copies[2].wait()
    copies[3].wait()


def entry(out_grad, inputs, preact, w_down, outer, narrow_n):
    rows, cols = out_grad.shape
    tokens = rows * 4 * outer
    hidden = preact.shape[1]
    slots = 4 * (2 * outer - 1)
    vmem, anywhere = (pl.BlockSpec(memory_space=space) for space in (pltpu.VMEM, pl.ANY))
    return pl.pallas_call(
        functools.partial(entry_kernel, outer, narrow_n),
        out_shape=(
            jax.ShapeDtypeStruct((tokens, cols), BF16),
            jax.ShapeDtypeStruct((tokens, cols), BF16),
            jax.ShapeDtypeStruct((tokens, hidden), BF16),
            jax.ShapeDtypeStruct((tokens, hidden), F32),
            jax.ShapeDtypeStruct((tokens, hidden), BF16),
        ),
        in_specs=[vmem, vmem, vmem, anywhere],
        out_specs=(vmem, anywhere, anywhere, vmem, vmem),
        scratch_shapes=[
            pltpu.VMEM(w_down.shape, BF16),
            pltpu.SemaphoreType.DMA((2, slots)),
            pltpu.SemaphoreType.DMA((2, slots)),
            pltpu.SemaphoreType.DMA((narrow_n,)),
            pltpu.SemaphoreType.DMA((narrow_n,)),
            pltpu.SemaphoreType.DMA((4,)),
        ],
        compiler_params=pltpu.CompilerParams(
            collective_id=0, has_side_effects=True, vmem_limit_bytes=56 * 2**20
        ),
    )(out_grad, inputs, preact, w_down)


def shift_narrow(x, s, n):
    return lax.ppermute(x, "narrow", [(i, (i + s) % n) for i in range(n)])


def scatter_chunk(part, k, outer, per):
    wide = lax.axis_index("wide")
    o, m, c = wide // 4, (wide // 2) % 2, wide % 2
    rows, cols = part.shape[-2:]
    low = part.astype(BF16)
    keep = lax.dynamic_index_in_dim(part, c, 2, keepdims=False)
    give = lax.dynamic_index_in_dim(low, 1 - c, 2, keepdims=False)
    got = lax.ppermute(give, "wide", [(i, i ^ 1) for i in range(4 * outer)])
    chip = keep + got.astype(F32)
    keep = lax.dynamic_index_in_dim(chip, m, 1, keepdims=False)
    give = lax.dynamic_index_in_dim(chip.astype(BF16), 1 - m, 1, keepdims=False)
    got = lax.ppermute(give, "wide", [(i, i ^ 2) for i in range(4 * outer)])
    pair = keep + got.astype(F32)
    low = pair.astype(BF16)
    first = k * per
    total = lax.dynamic_index_in_dim(pair, jnp.clip(o - first, 0, per - 1), 0, keepdims=False)
    for s in range(1, outer):
        target = jnp.clip(lax.rem(o - s + outer, outer) - first, 0, per - 1)
        give = lax.dynamic_index_in_dim(low, target, 0, keepdims=False)
        pairs = [
            (place((d + s) % outer, a, b), place(d, a, b))
            for d in range(first, first + per)
            for a in range(2)
            for b in range(2)
        ]
        total = total + lax.ppermute(give, "wide", pairs).astype(F32)
    return total


def outer_product_kernel(a_ref, b_ref, o_ref):
    o_ref[...] = lax.dot_general(
        a_ref[...], b_ref[...], (((0,), (0,)), ((), ())), preferred_element_type=F32
    ).astype(BF16)


def outer_product(a, b):
    t, d = a.shape
    f = b.shape[1]
    tile = min(256, d)
    return pl.pallas_call(
        outer_product_kernel,
        grid=(d // tile,),
        in_specs=[
            pl.BlockSpec((t, tile), lambda i: (0, i)),
            pl.BlockSpec((t, f), lambda i: (0, 0)),
        ],
        out_specs=pl.BlockSpec((tile, f), lambda i: (i, 0)),
        out_shape=jax.ShapeDtypeStruct((d, f), BF16),
        compiler_params=pltpu.CompilerParams(vmem_limit_bytes=40 * 2**20),
        cost_estimate=pl.CostEstimate(
            flops=2 * t * d * f,
            bytes_accessed=2 * (t * d + t * f + d * f),
            transcendentals=0,
        ),
    )(a, b)


def shards(inputs, out_grad, preact, w_up, w_down):
    wide_n = lax.axis_size("wide")
    narrow_n = lax.axis_size("narrow")
    outer = wide_n // 4
    tokens = preact.shape[0] * narrow_n

    grad_all, inputs_all, pre_all, part_all, low_all = entry(
        out_grad, inputs, preact, w_down, outer, narrow_n
    )
    span = tokens // CHUNKS
    acts = []
    for k in range(CHUNKS):
        rows_k = slice(k * span, (k + 1) * span)
        low = low_all[rows_k]
        acts.append(
            (part_all[rows_k], [shift_narrow(low, s, narrow_n) for s in range(1, narrow_n)])
        )
    activ = gelu_parts(pre_all)[0].astype(BF16)
    down_grad = outer_product(activ, grad_all)

    pgrads, totals = [], []
    per = outer // CHUNKS
    for k, (part, others) in enumerate(acts):
        act = part
        if totals:
            act, others, _ = lax.optimization_barrier((part, others, prod))
        for other in others:
            act = act + other.astype(F32)
        slope = gelu_parts(pre_all[k * span : (k + 1) * span])[1]
        pgrad = (act * slope).astype(BF16)
        pgrads.append(pgrad)
        prod = lax.dot_general(
            pgrad, w_up, (((1,), (1,)), ((), ())), preferred_element_type=F32
        )
        totals.append(
            scatter_chunk(prod.reshape(per, 2, 2, -1, prod.shape[1]), k, outer, per)
        )
    up_grad = outer_product(inputs_all, jnp.concatenate(pgrads, 0))
    o = lax.axis_index("wide") // 4
    in_grad = totals[0]
    for k in range(1, CHUNKS):
        in_grad = jnp.where(o >= k * per, totals[k], in_grad)
    return (in_grad.astype(BF16), up_grad, down_grad)


def solution(mesh):
    in_specs = (
        P("wide", "narrow"),
        P("wide", "narrow"),
        P("narrow", "wide"),
        P("narrow", "wide"),
        P("wide", "narrow"),
    )
    out_specs = (P("wide", "narrow"), P("narrow", "wide"), P("wide", "narrow"))
    return jax.shard_map(shards, mesh=mesh, in_specs=in_specs, out_specs=out_specs, check_vma=False)
```
